32 devices in a mesh: groups: 2 (over y), expert: 8 (over z, core), attn: 2 (over x).
Axes of the slice: x: 2, y: 2, z: 4, core: 2. Of those that a mesh axis runs over, the one named last changes fastest.
Arguments:
- tokens: bfloat16 [512, 3584], P(('groups', 'expert')), parts along dimension 0, may hold values from -6 to 6
- gates: float32 [512, 8], P(('groups', 'expert')), parts along dimension 0, may hold values from 0.05 to 0.6
- slots: int32 [512, 8], P(('groups', 'expert')), parts along dimension 0, may hold values from 0 to 15, all different within a row; in each aligned block of 32 rows (0 to 31, 32 to 63, ...) at most 20 rows name the same one
- plan: int32 [16], P('groups'), parts along dimension 0, may hold values from 0 to 7, as said below
- gate_proj: bfloat16 [8, 3584, 1024], P('expert', None, 'attn'), may hold values from -0.09375 to 0.09375
- up_proj: bfloat16 [8, 3584, 1024], P('expert', None, 'attn'), may hold values from -0.09375 to 0.09375
- down_proj: bfloat16 [8, 3584, 1024], P('expert', None, 'attn'), may hold values from -0.1875 to 0.1875
Outputs:
- moe_out: bfloat16 [512, 3584], P(('groups', 'expert')), parts along dimension 0
The draws below stay inside these ranges and needn't reach their ends.
There are 2 independent parts, one for each index of `groups`. The reference program is written for one: setup_inputs(seed, part) draws one part's arguments, and reference() takes and returns one part's arrays. A program takes and returns all parts, laid end to end along the dimension named above; an argument that names none is the same for every part. Nothing has to cross between parts.
Inputs may be any that keep to these rules, and one draw needn't show every extreme that they name: A row's 8 slots are distinct; among the 32 rows of one index of expert (aligned blocks) no slot is named more than 20 times, a bound that some block reaches. plan[d] is never d; no expert is named by more than 2 entries of plan, and some expert by exactly 2.
All inputs are finite; a program needn't handle non-finite values.
Results may differ from the reference program's by a relative error of at most 0.014.
Values may be sent and summed in bfloat16 or wider, within the bound.
No kernel may reach another device: no remote copies, remote signals or barrier semaphores. Data moves between devices by JAX's collectives and lax.ppermute only.
A program may use at most 128 MiB of HBM per device.

```python
import math
import jax
import jax.numpy as jnp
import numpy as np
from jax import lax

D = 3584
FF = 1024
TOP = 8
TOK_DEV = 32
TOKENS = 256
EXPERTS = 8
SPARES = 8
SLOTS = 16
CAP = 20
N_EXPERT = 8
N_ATTN = 2


def draw_plan(key, part):
    order = jax.random.permutation(jax.random.fold_in(key, 11), SPARES).astype(jnp.int32)
    index = jnp.arange(SPARES, dtype=jnp.int32)
    half = SPARES // 2
    target = jnp.where(index < half, index // 2 * 2 + 2, (index + 1) % SPARES)
    result = jnp.zeros((SPARES,), jnp.int32).at[order].set(order[target])
    return result


def levels(stream_key, shape, shards, low, high):
    loudness = 1.0
    for axis_at, blocks in shards:
        draws = jax.random.uniform(jax.random.fold_in(jax.random.fold_in(stream_key, 6), axis_at), (blocks,), jnp.float32, low / len(shards), high / len(shards))
        loudness = loudness * jnp.repeat(jnp.exp(draws), shape[axis_at] // blocks).reshape((-1,) + (1,) * (len(shape) - 1 - axis_at))
    return loudness


def routed_block(rng, own, number, rows, count, top, limit, slope):
    order = jax.random.permutation(rng, count)
    packed, usual = portions_of(count, rows * top, limit, slope, True), portions_of(count, rows * top, limit, slope, False)
    places = jnp.arange(count)

    def named(lengths, rotation):
        used = int((lengths > 0).sum())
        fixed = max(1, used // 4)
        moved = fixed + (places - fixed + rotation * (used - fixed)) % max(1, count - fixed)
        return jnp.zeros((count,), jnp.int32).at[order[jnp.where(places < fixed, places, moved)]].set(jnp.asarray(lengths, jnp.int32))

    lengths = jnp.where(number % 4 == 0, named(packed, number // 4), named(usual, number - number // 4 - 1))
    mixed = jax.random.permutation(jax.random.fold_in(own, 3), count)
    giver, taker = mixed[0:count // 2 * 2:2], mixed[1:count // 2 * 2:2]
    margin = jnp.minimum(lengths[giver] - 1, limit - lengths[taker]) // 2
    margin = jnp.where((giver == order[0]) | (taker == order[0]) | (lengths[taker] == 0), 0, jnp.maximum(margin, 0))
    moved = jax.random.randint(jax.random.fold_in(own, 4), (count // 2,), 0, 1 << 20) % (margin + 1)
    lengths = lengths.at[giver].add(-moved).at[taker].add(moved)
    labels = jnp.searchsorted(jnp.cumsum(lengths), jnp.arange(rows * top), side="right").astype(jnp.int32)
    table = labels.reshape(top, rows).T
    table = table[jax.random.permutation(jax.random.fold_in(own, 1), rows)]
    rotation = jax.random.randint(jax.random.fold_in(own, 2), (rows, 1), 0, top)
    return jnp.take_along_axis(table, (jnp.arange(top)[None, :] + rotation) % top, axis=1)


def portions_of(amount, total, limit, skew, full):
    portions = [(1 << 20) // math.isqrt(grade ** skew) + 1 for grade in range(1, amount + 1)]
    largest = limit if full else min(limit, max(-(-total // amount), total * portions[0] // sum(portions)))
    least = 1 if total - largest >= amount - 1 else 0
    counts, spare = [largest] + [least] * (amount - 1), total - largest - least * (amount - 1)
    while spare > 0:
        free = [i for i in range(1, amount) if counts[i] < largest] or [i for i in range(1, amount) if counts[i] < limit]
        whole, budget = sum([portions[i] for i in free]), spare
        for i in free:
            more = min(limit - counts[i], max(1, budget * portions[i] // whole), spare)
            counts[i] = counts[i] + more
            spare = spare - more
    return np.array(counts)


def noise(key, extent, deviation, reach, pieces=(), kind=jnp.bfloat16):
    drawn = deviation * jax.random.normal(key, extent, jnp.float32)
    if pieces:
        drawn = drawn * levels(key, extent, pieces, -0.22, 0.18)
    return jnp.clip(drawn, -reach, reach).astype(kind)


def setup_inputs(seed: int = 0, part: int = 0) -> dict:
    streams_of = jax.random.split(jax.random.key(seed), 8)
    part_splits = jax.random.split(jax.random.fold_in(streams_of[7], part), 8)
    tokens = noise(part_splits[0], (TOKENS, D), 1.0, 6.0, ((0, 8),))
    gates = jnp.clip(jnp.exp(math.log(0.6) - 2.4849067 * jax.random.uniform(part_splits[1], (TOKENS, TOP), jnp.float32) ** levels(part_splits[1], (TOKENS, TOP), ((0, 8),), -0.2, 0.2)), 0.05, 0.6)
    slots_keys = jax.random.split(jax.random.fold_in(part_splits[2], 1), TOKENS // TOK_DEV)
    slots_turns = jax.random.permutation(jax.random.fold_in(part_splits[2], 3), TOKENS // TOK_DEV)
    slots = jax.vmap(lambda own, number: routed_block(jax.random.fold_in(part_splits[2], 2), own, number, TOK_DEV, SLOTS, TOP, CAP, 1))(slots_keys, slots_turns).reshape((TOKENS, TOP))
    plan = draw_plan(jax.random.fold_in(jax.random.fold_in(streams_of[7], part), 71), part)
    gate_proj = noise(streams_of[4], (EXPERTS, D, FF), D ** -0.5, 0.09375, ((0, 8), (2, 2)))
    up_proj = noise(streams_of[5], (EXPERTS, D, FF), D ** -0.5, 0.09375, ((0, 8), (2, 2)))
    down_proj = noise(streams_of[6], (EXPERTS, D, FF), FF ** -0.5, 0.1875, ((0, 8), (2, 2)))
    return dict(tokens=tokens, gates=gates, slots=slots, plan=plan, gate_proj=gate_proj, up_proj=up_proj, down_proj=down_proj)


def expert_rows(rows, w_gate, w_up, w_down):
    rows_float = rows.astype(jnp.float32)
    gate_act = jnp.dot(rows_float, w_gate.astype(jnp.float32), precision=lax.Precision.HIGHEST)
    up_act = jnp.dot(rows_float, w_up.astype(jnp.float32), precision=lax.Precision.HIGHEST)
    hidden = (jax.nn.silu(gate_act) * up_act).astype(jnp.bfloat16)
    row_count = rows.shape[0]
    group = FF // N_ATTN
    hidden_split = hidden.astype(jnp.float32).reshape(row_count, N_ATTN, group)
    down_split = w_down.astype(jnp.float32).reshape(D, N_ATTN, group)
    down_part = jnp.einsum("rap,dap->rad", hidden_split, down_split, precision=lax.Precision.HIGHEST)
    down_part = lax.optimization_barrier(down_part.astype(jnp.bfloat16))
    return jnp.sum(down_part.astype(jnp.float32), axis=1)


def reference(tokens, gates, slots, plan, gate_proj, up_proj, down_proj):
    slot_ids = jnp.arange(2 * N_EXPERT, dtype=jnp.int32)
    expert_of = jnp.where(slot_ids % 2 == 0, slot_ids // 2, plan[slot_ids // 2]).astype(jnp.int32)
    per_block = TOK_DEV * TOP
    pair_slots = slots.reshape(N_EXPERT, per_block).astype(jnp.int32)
    onehot = (pair_slots[:, :, None] == slot_ids[None, None, :]).astype(jnp.int32)
    running = jnp.cumsum(onehot, axis=1)
    position = (jnp.sum(running * onehot, axis=2) - 1).astype(jnp.int32)
    block_index = jnp.broadcast_to(jnp.arange(N_EXPERT, dtype=jnp.int32)[:, None], (N_EXPERT, per_block))
    local_token = jnp.broadcast_to((jnp.arange(per_block, dtype=jnp.int32) // TOP)[None, :], (N_EXPERT, per_block))
    token_table = jnp.zeros((2 * N_EXPERT, N_EXPERT, CAP), jnp.int32)
    token_table = token_table.at[pair_slots, block_index, position].set(local_token + block_index * TOK_DEV)

    def one_slot(slot):
        expert = expert_of[slot]
        rows = tokens[token_table[slot].reshape(-1)]
        result = expert_rows(rows, gate_proj[expert], up_proj[expert], down_proj[expert])
        return result.reshape(N_EXPERT, CAP, D)

    outputs = lax.map(one_slot, slot_ids)
    picked = outputs[pair_slots, block_index, position]
    picked = picked.reshape(N_EXPERT * TOK_DEV, TOP, D)
    total = jnp.sum(picked * gates[:, :, None], axis=1)
    return total.astype(jnp.bfloat16)
```

```python
import functools

import jax
import jax.numpy as jnp
from jax import lax
from jax.experimental import pallas as pl
from jax.experimental.pallas import tpu as pltpu
from jax.sharding import PartitionSpec as P

LANES = 128
VMEM = pl.BlockSpec(memory_space=pltpu.VMEM)
SMEM = pl.BlockSpec(memory_space=pltpu.SMEM)


def expert_weights(slots, gates, plan_ref, experts):
    owner = slots >> 1
    copied = jnp.zeros_like(slots)
    for d in range(experts):
        copied = jnp.where(owner == d, plan_ref[d], copied)
    chosen = jnp.where((slots & 1) == 0, owner, copied)
    return [
        jnp.sum(jnp.where(chosen == e, gates, 0.0), axis=0, keepdims=True)
        for e in range(experts)
    ]


def prepare_kernel(experts, at_ref, plan_ref, slots_ref, gates_ref, tok_ref, all_ref, mine_ref, w_ref):
    count, width = tok_ref.shape
    half = count // 2
    sums = expert_weights(slots_ref[...], gates_ref[...], plan_ref, experts)
    high = [s.astype(jnp.bfloat16).astype(jnp.float32) for s in sums]
    low = [s - h for s, h in zip(sums, high)]
    pad = jnp.zeros((LANES - 2 * experts, count), jnp.float32)
    table = jnp.concatenate(high + low + [pad], axis=0)
    table = jnp.concatenate([table, jnp.zeros((LANES, LANES - count), jnp.float32)], axis=1)
    w_ref[...] = table.T[:count]
    for place in range(2):
        start = pl.multiple_of((at_ref[0] ^ place) * half, half)
        rows = tok_ref[pl.ds(start, half), :]
        weights = w_ref[pl.ds(start, half), :].astype(jnp.bfloat16)
        here = pl.ds(place * half, half)
        all_ref[here, pl.ds(0, width)] = rows
        all_ref[here, pl.ds(width, LANES)] = weights
        if place == 0:
            mine_ref[:, pl.ds(0, width)] = rows
            mine_ref[:, pl.ds(width, LANES)] = weights


def prepare(tokens, gates, slots, plan, experts, attn_at):
    count, width = tokens.shape
    return pl.pallas_call(
        functools.partial(prepare_kernel, experts),
        out_shape=(
            jax.ShapeDtypeStruct((count, width + LANES), jnp.bfloat16),
            jax.ShapeDtypeStruct((count // 2, width + LANES), jnp.bfloat16),
        ),
        in_specs=[SMEM, SMEM, VMEM, VMEM, VMEM],
        out_specs=(VMEM, VMEM),
        scratch_shapes=[pltpu.VMEM((count, LANES), jnp.float32)],
        name="prepare",
    )(attn_at.reshape(1), plan, slots.T, gates.T, tokens)


def ffn_kernel(experts, blocks, at_ref, *refs):
    x_refs = refs[:blocks]
    gate_ref, up_ref, down_ref, keep_ref, send_ref, x_ref, h_ref, w_ref = refs[blocks:]
    width, units = gate_ref.shape
    row = 0
    for ref in x_refs:
        size = ref.shape[0]
        x_ref[pl.ds(row, size), :] = ref[:, pl.ds(0, width)]
        w_ref[pl.ds(row, size), :] = ref[:, pl.ds(width, LANES)].astype(jnp.float32)
        row += size
    lane = lax.broadcasted_iota(jnp.int32, (1, LANES), 1)
    own = (lane == at_ref[0]) | (lane == at_ref[0] + experts)
    weight = jnp.sum(jnp.where(own, w_ref[...], 0.0), axis=1, keepdims=True)
    w_ref[...] = jnp.broadcast_to(weight, w_ref.shape)
    tile = min(256, units)
    for n in range(0, units, tile):
        cols = pl.ds(n, tile)
        gate = jnp.dot(x_ref[...], gate_ref[:, cols], preferred_element_type=jnp.float32)
        up = jnp.dot(x_ref[...], up_ref[:, cols], preferred_element_type=jnp.float32)
        h_ref[:, cols] = (gate / (1.0 + jnp.exp(-gate)) * up).astype(jnp.bfloat16)
    half = row // 2
    wide = 512

    def down(j, carry):
        cols = pl.ds(pl.multiple_of(j * wide, wide), wide)
        y = lax.dot_general(
            h_ref[...], down_ref[cols, :], (((1,), (1,)), ((), ())), preferred_element_type=jnp.float32
        )
        y = (y * w_ref[:, pl.ds(0, 1)]).astype(jnp.bfloat16)
        keep_ref[:, cols] = y[:half]
        send_ref[:, cols] = y[half:]
        return carry

    lax.fori_loop(0, width // wide, down, 0)


def ffn(x_blocks, w_gate, w_up, w_down, expert_at, experts):
    width, units = w_gate.shape
    rows = sum(b.shape[0] for b in x_blocks)
    out = jax.ShapeDtypeStruct((rows // 2, width), jnp.bfloat16)
    return pl.pallas_call(
        functools.partial(ffn_kernel, experts, len(x_blocks)),
        out_shape=(out, out),
        in_specs=[SMEM] + [VMEM] * (len(x_blocks) + 3),
        out_specs=(VMEM, VMEM),
        scratch_shapes=[
            pltpu.VMEM((rows, width), jnp.bfloat16),
            pltpu.VMEM((rows, units), jnp.bfloat16),
            pltpu.VMEM((rows, LANES), jnp.float32),
        ],
        cost_estimate=pl.CostEstimate(
            flops=6 * rows * width * units,
            bytes_accessed=6 * width * units + 8 * rows * width,
            transcendentals=rows * units,
        ),
        name="ffn",
    )(expert_at.reshape(1), *x_blocks, w_gate, w_up, w_down)


def add(*terms):
    total = terms[0].astype(jnp.float32)
    for term in terms[1:]:
        total = total + term.astype(jnp.float32)
    return total.astype(jnp.bfloat16)


def body_line(tokens, gates, slots, plan, gate_proj, up_proj, down_proj):
    experts = lax.axis_size("expert")
    expert_at = lax.axis_index("expert").astype(jnp.int32)
    attn_at = lax.axis_index("attn").astype(jnp.int32)
    half = tokens.shape[0] // 2

    def swap(value, bit):
        return lax.ppermute(value, "expert", [(i, i ^ bit) for i in range(experts)])

    def core(value):
        return swap(value, 1)

    def pair(value):
        return lax.ppermute(value, "attn", [(0, 1), (1, 0)])

    own, mine = prepare(tokens, gates, slots, plan, experts, attn_at)
    weights = (gate_proj[0], up_proj[0], down_proj[0])

    own_core = core(own)
    far = [swap(mine, 2 * k) for k in (3, 2)]
    near = swap(own, 2)
    near_core = core(near)
    far_rows = []
    for block in far:
        other = pair(block)
        far_rows.append(([block, other], [core(block), core(other)]))

    keep, send = ffn([own, near, own_core, near_core], *weights, expert_at, experts)
    count = 2 * half
    got = core(send)
    near_sum = swap(add(keep[count:], got[count:]), 2)
    both = add(keep[:count], got[:count], near_sum)
    terms = [both[:half], pair(both[half:])]
    for k, (kept, sent) in zip((3, 2), far_rows):
        keep, send = ffn(kept + sent, *weights, expert_at, experts)
        got = core(send)
        total = add(keep, got)
        part = add(total[:half], pair(total[half:]))
        terms.append(swap(part, 2 * k))
    final = add(*terms)
    other = pair(final)
    return jnp.where(
        attn_at == 0,
        jnp.concatenate([final, other], axis=0),
        jnp.concatenate([other, final], axis=0),
    )


def body_any(tokens, gates, slots, plan, gate_proj, up_proj, down_proj):
    experts = lax.axis_size("expert")
    expert_at = lax.axis_index("expert").astype(jnp.int32)
    owner = slots >> 1
    chosen = jnp.where((slots & 1) == 0, owner, plan[owner])
    hit = chosen[:, :, None] == jnp.arange(experts, dtype=jnp.int32)
    sums = jnp.sum(jnp.where(hit, gates[:, :, None], 0.0), axis=1)
    rows = lax.all_gather(tokens, "expert", axis=0, tiled=True)
    weight = lax.all_gather(sums, "expert", axis=0, tiled=True)
    weight = jnp.sum(
        jnp.where(jnp.arange(experts, dtype=jnp.int32) == expert_at, weight, 0.0), axis=1
    )
    gate = jnp.dot(rows, gate_proj[0], preferred_element_type=jnp.float32)
    up = jnp.dot(rows, up_proj[0], preferred_element_type=jnp.float32)
    hidden = (jax.nn.silu(gate) * up).astype(jnp.bfloat16)
    down = jnp.einsum("rf,df->rd", hidden, down_proj[0], preferred_element_type=jnp.float32)
    part = (down * weight[:, None]).astype(jnp.bfloat16)
    mine = lax.psum_scatter(part, "expert", scatter_dimension=0, tiled=True)
    return lax.psum(mine, "attn")


def solution(mesh):
    sizes = dict(mesh.shape)
    line = sizes["attn"] == 2 and sizes["expert"] == 8
    return jax.shard_map(
        body_line if line else body_any,
        mesh=mesh,
        in_specs=(
            P(("groups", "expert"), None),
            P(("groups", "expert"), None),
            P(("groups", "expert"), None),
            P("groups"),
            P("expert", None, "attn"),
            P("expert", None, "attn"),
            P("expert", None, "attn"),
        ),
        out_specs=P(("groups", "expert"), None),
        check_vma=False,
    )
```

```python
import functools

import jax
import jax.numpy as jnp
from jax import lax
from jax.experimental import pallas as pl
from jax.experimental.pallas import tpu as pltpu
from jax.sharding import PartitionSpec as P

LANES = 128
SMALL = 4 << 20
VMEM = pl.BlockSpec(memory_space=pltpu.VMEM)
SMEM = pl.BlockSpec(memory_space=pltpu.SMEM)


def expert_weights(slots, gates, plan_ref, experts):
    owner = slots >> 1
    copied = jnp.zeros_like(slots)
    for d in range(experts):
        copied = jnp.where(owner == d, plan_ref[d], copied)
    chosen = jnp.where((slots & 1) == 0, owner, copied)
    return [
        jnp.sum(jnp.where(chosen == e, gates, 0.0), axis=0, keepdims=True)
        for e in range(experts)
    ]


def prepare_kernel(
    experts, at_ref, expert_ref, plan_hbm, slots_hbm, gates_hbm, tok_hbm, all_ref, mine_ref,
    plan_ref, slots_ref, gates_ref, w_ref, sems
):
    count, width = tok_hbm.shape
    half = count // 2
    copies = [
        pltpu.make_async_copy(plan_hbm, plan_ref, sems.at[0]),
        pltpu.make_async_copy(slots_hbm, slots_ref, sems.at[1]),
        pltpu.make_async_copy(gates_hbm, gates_ref, sems.at[2]),
    ]
    starts = [pl.multiple_of((at_ref[0] ^ place) * half, half) for place in range(2)]
    targets = [
        (starts[0], mine_ref.at[:, pl.ds(0, width)]),
        (starts[0], all_ref.at[pl.ds(0, half), pl.ds(0, width)]),
        (starts[1], all_ref.at[pl.ds(half, half), pl.ds(0, width)]),
    ]
    for i, (start, target) in enumerate(targets):
        copies.append(pltpu.make_async_copy(tok_hbm.at[pl.ds(start, half), :], target, sems.at[3 + i]))
    for copy in copies:
        copy.start()
    for copy in copies[:3]:
        copy.wait()
    sums = expert_weights(slots_ref[...], gates_ref[...], plan_ref, experts)
    high = [s.astype(jnp.bfloat16).astype(jnp.float32) for s in sums]
    low = [s - h for s, h in zip(sums, high)]
    pad = jnp.zeros((LANES - 2 * experts, count), jnp.float32)
    table = jnp.concatenate(high + low + [pad], axis=0)
    table = jnp.concatenate([table, jnp.zeros((LANES, LANES - count), jnp.float32)], axis=1)
    w_ref[...] = table.T[:count]
    for place in range(2):
        weights = w_ref[pl.ds(starts[place], half), :].astype(jnp.bfloat16)
        all_ref[pl.ds(place * half, half), pl.ds(width, LANES)] = weights
        if place == 0:
            mine_ref[:, pl.ds(width, LANES)] = weights
    for copy in copies[3:]:
        copy.wait()


def prepare(tokens, gates, slots, plan, experts, attn_at, expert_at):
    count, width = tokens.shape
    top = slots.shape[1]
    given = [pltpu.with_memory_space_constraint(v, pltpu.HBM) for v in (plan, slots.T, gates.T, tokens)]
    return pl.pallas_call(
        functools.partial(prepare_kernel, experts),
        out_shape=(
            jax.ShapeDtypeStruct((count, width + LANES), jnp.bfloat16),
            jax.ShapeDtypeStruct((count // 2, width + LANES), jnp.bfloat16),
        ),
        in_specs=[SMEM] * 2 + [pl.BlockSpec(memory_space=pltpu.HBM)] * 4,
        out_specs=(VMEM, VMEM),
        scratch_shapes=[
            pltpu.SMEM((experts,), jnp.int32),
            pltpu.VMEM((top, count), jnp.int32),
            pltpu.VMEM((top, count), jnp.float32),
            pltpu.VMEM((count, LANES), jnp.float32),
            pltpu.SemaphoreType.DMA((6,)),
        ],
        compiler_params=pltpu.CompilerParams(vmem_limit_bytes=SMALL),
        name="prepare",
    )(attn_at.reshape(1), expert_at.reshape(1), *given)


def load_kernel(*refs):
    count = len(refs) // 2
    sources, targets, sems = refs[:count], refs[count : 2 * count], refs[-1]
    copies = [
        pltpu.make_async_copy(source, target, sems.at[i])
        for i, (source, target) in enumerate(zip(sources, targets))
    ]
    for copy in copies:
        copy.start()
    for copy in copies:
        copy.wait()


def load(*arrays):
    return pl.pallas_call(
        load_kernel,
        out_shape=tuple(jax.ShapeDtypeStruct(a.shape, a.dtype) for a in arrays),
        in_specs=[pl.BlockSpec(memory_space=pltpu.HBM)] * len(arrays),
        out_specs=(VMEM,) * len(arrays),
        scratch_shapes=[pltpu.SemaphoreType.DMA((len(arrays),))],
        compiler_params=pltpu.CompilerParams(vmem_limit_bytes=SMALL),
        cost_estimate=pl.CostEstimate(
            flops=0, transcendentals=0, bytes_accessed=sum(2 * a.size * a.dtype.itemsize for a in arrays)
        ),
        name="load",
    )(*[pltpu.with_memory_space_constraint(a, pltpu.HBM) for a in arrays])


def ffn_kernel(experts, blocks, at_ref, *refs):
    x_refs = refs[:blocks]
    gate_ref, up_ref, down_ref, keep_ref, send_ref, x_ref, h_ref, w_ref = refs[blocks:]
    width, units = gate_ref.shape
    row = 0
    for ref in x_refs:
        size = ref.shape[0]
        x_ref[pl.ds(row, size), :] = ref[:, pl.ds(0, width)]
        w_ref[pl.ds(row, size), :] = ref[:, pl.ds(width, LANES)].astype(jnp.float32)
        row += size
    lane = lax.broadcasted_iota(jnp.int32, (1, LANES), 1)
    own = (lane == at_ref[0]) | (lane == at_ref[0] + experts)
    weight = jnp.sum(jnp.where(own, w_ref[...], 0.0), axis=1, keepdims=True)
    w_ref[...] = jnp.broadcast_to(weight, w_ref.shape)
    tile = min(256, units)
    for n in range(0, units, tile):
        cols = pl.ds(n, tile)
        gate = jnp.dot(x_ref[...], gate_ref[:, cols], preferred_element_type=jnp.float32)
        up = jnp.dot(x_ref[...], up_ref[:, cols], preferred_element_type=jnp.float32)
        h_ref[:, cols] = (gate / (1.0 + jnp.exp(-gate)) * up).astype(jnp.bfloat16)
    half = row // 2
    wide = 512

    def down(j, carry):
        cols = pl.ds(pl.multiple_of(j * wide, wide), wide)
        y = lax.dot_general(
            h_ref[...], down_ref[cols, :], (((1,), (1,)), ((), ())), preferred_element_type=jnp.float32
        )
        y = (y * w_ref[:, pl.ds(0, 1)]).astype(jnp.bfloat16)
        keep_ref[:, cols] = y[:half]
        send_ref[:, cols] = y[half:]
        return carry

    lax.fori_loop(0, width // wide, down, 0)


def ffn(x_blocks, w_gate, w_up, w_down, expert_at, experts):
    width, units = w_gate.shape
    rows = sum(b.shape[0] for b in x_blocks)
    out = jax.ShapeDtypeStruct((rows // 2, width), jnp.bfloat16)
    return pl.pallas_call(
        functools.partial(ffn_kernel, experts, len(x_blocks)),
        out_shape=(out, out),
        in_specs=[SMEM] + [VMEM] * (len(x_blocks) + 3),
        out_specs=(VMEM, VMEM),
        scratch_shapes=[
            pltpu.VMEM((rows, width), jnp.bfloat16),
            pltpu.VMEM((rows, units), jnp.bfloat16),
            pltpu.VMEM((rows, LANES), jnp.float32),
        ],
        cost_estimate=pl.CostEstimate(
            flops=6 * rows * width * units,
            bytes_accessed=6 * width * units + 8 * rows * width,
            transcendentals=rows * units,
        ),
        compiler_params=pltpu.CompilerParams(vmem_limit_bytes=2 * SMALL),
        name="ffn",
    )(expert_at.reshape(1), *x_blocks, w_gate, w_up, w_down)


def add(*terms):
    total = terms[0].astype(jnp.float32)
    for term in terms[1:]:
        total = total + term.astype(jnp.float32)
    return total.astype(jnp.bfloat16)


def body_line(tokens, gates, slots, plan, gate_proj, up_proj, down_proj):
    return line(tokens, gates, slots, plan, gate_proj, up_proj, down_proj)


def line(tokens, gates, slots, plan, gate_proj, up_proj, down_proj):
    experts = lax.axis_size("expert")
    expert_at = lax.axis_index("expert").astype(jnp.int32)
    attn_at = lax.axis_index("attn").astype(jnp.int32)
    count = tokens.shape[0]
    half = count // 2

    def swap(value, bit):
        return lax.ppermute(value, "expert", [(i, i ^ bit) for i in range(experts)])

    def core(value):
        return swap(value, 1)

    def pair(value):
        return lax.ppermute(value, "attn", [(0, 1), (1, 0)])

    def run(*blocks):
        return ffn(blocks, *weights, expert_at, experts)

    own, mine = prepare(tokens, gates, slots, plan, experts, attn_at, expert_at)
    far = swap(mine, 4)
    near = swap(own, 2)
    own_core = core(own)
    weights = load(gate_proj[0], up_proj[0], down_proj[0])

    relay = swap(far, 2)
    far_pair = pair(far)
    far_core = core(far)
    near_core = core(near)
    keep, send = run(own, near, own_core, near_core)
    got = core(send)
    relay_pair = pair(relay)
    relay_core = core(relay)
    far_pair_core = core(far_pair)
    far_keep, far_send = run(far, far_pair, far_core, far_pair_core)
    far_got = core(far_send)
    near_sum = swap(add(keep[count:], got[count:]), 2)
    relay_pair_core = core(relay_pair)
    far_total = add(far_keep, far_got)
    far_other = pair(far_total[half:])
    relay_keep, relay_send = run(relay, relay_pair, relay_core, relay_pair_core)
    relay_got = core(relay_send)
    relay_total = add(relay_keep, relay_got)
    relay_other = pair(relay_total[half:])
    relay_sum = swap(add(relay_total[:half], relay_other), 2)
    far_sum = swap(add(far_total[:half], far_other, relay_sum), 4)
    both = add(keep[:count], got[:count], near_sum)
    near_other = pair(both[half:])
    final = add(both[:half], near_other, far_sum)
    other = pair(final)
    return jnp.where(
        attn_at == 0,
        jnp.concatenate([final, other], axis=0),
        jnp.concatenate([other, final], axis=0),
    )


def body_any(tokens, gates, slots, plan, gate_proj, up_proj, down_proj):
    experts = lax.axis_size("expert")
    expert_at = lax.axis_index("expert").astype(jnp.int32)
    owner = slots >> 1
    chosen = jnp.where((slots & 1) == 0, owner, plan[owner])
    hit = chosen[:, :, None] == jnp.arange(experts, dtype=jnp.int32)
    sums = jnp.sum(jnp.where(hit, gates[:, :, None], 0.0), axis=1)
    rows = lax.all_gather(tokens, "expert", axis=0, tiled=True)
    weight = lax.all_gather(sums, "expert", axis=0, tiled=True)
    weight = jnp.sum(
        jnp.where(jnp.arange(experts, dtype=jnp.int32) == expert_at, weight, 0.0), axis=1
    )
    gate = jnp.dot(rows, gate_proj[0], preferred_element_type=jnp.float32)
    up = jnp.dot(rows, up_proj[0], preferred_element_type=jnp.float32)
    hidden = (jax.nn.silu(gate) * up).astype(jnp.bfloat16)
    down = jnp.einsum("rf,df->rd", hidden, down_proj[0], preferred_element_type=jnp.float32)
    part = (down * weight[:, None]).astype(jnp.bfloat16)
    mine = lax.psum_scatter(part, "expert", scatter_dimension=0, tiled=True)
    return lax.psum(mine, "attn")


def solution(mesh):
    sizes = dict(mesh.shape)
    line_form = sizes["attn"] == 2 and sizes["expert"] == 8
    return jax.shard_map(
        body_line if line_form else body_any,
        mesh=mesh,
        in_specs=(
            P(("groups", "expert"), None),
            P(("groups", "expert"), None),
            P(("groups", "expert"), None),
            P("groups"),
            P("expert", None, "attn"),
            P("expert", None, "attn"),
            P("expert", None, "attn"),
        ),
        out_specs=P(("groups", "expert"), None),
        check_vma=False,
    )
```

```python
import functools

import jax
import jax.numpy as jnp
from jax import lax
from jax.experimental import pallas as pl
from jax.experimental.pallas import tpu as pltpu
from jax.sharding import PartitionSpec as P

LANES = 128
SMALL = 4 << 20
VMEM = pl.BlockSpec(memory_space=pltpu.VMEM)
SMEM = pl.BlockSpec(memory_space=pltpu.SMEM)


def expert_weights(slots, gates, plan_ref, experts):
    owner = slots >> 1
    copied = jnp.zeros_like(slots)
    for d in range(experts):
        copied = jnp.where(owner == d, plan_ref[d], copied)
    chosen = jnp.where((slots & 1) == 0, owner, copied)
    return [
        jnp.sum(jnp.where(chosen == e, gates, 0.0), axis=0, keepdims=True)
        for e in range(experts)
    ]


def prepare_kernel(
    experts, at_ref, expert_ref, plan_hbm, slots_hbm, gates_hbm, tok_hbm, all_ref, mine_ref,
    plan_ref, slots_ref, gates_ref, w_ref, sems
):
    count, width = tok_hbm.shape
    half = count // 2
    copies = [
        pltpu.make_async_copy(plan_hbm, plan_ref, sems.at[0]),
        pltpu.make_async_copy(slots_hbm, slots_ref, sems.at[1]),
        pltpu.make_async_copy(gates_hbm, gates_ref, sems.at[2]),
    ]
    starts = [pl.multiple_of((at_ref[0] ^ place) * half, half) for place in range(2)]
    targets = [
        (starts[0], mine_ref.at[:, pl.ds(0, width)]),
        (starts[0], all_ref.at[pl.ds(0, half), pl.ds(0, width)]),
        (starts[1], all_ref.at[pl.ds(half, half), pl.ds(0, width)]),
    ]
    for i, (start, target) in enumerate(targets):
        copies.append(pltpu.make_async_copy(tok_hbm.at[pl.ds(start, half), :], target, sems.at[3 + i]))
    for copy in copies:
        copy.start()
    for copy in copies[:3]:
        copy.wait()
    sums = expert_weights(slots_ref[...], gates_ref[...], plan_ref, experts)
    high = [s.astype(jnp.bfloat16).astype(jnp.float32) for s in sums]
    low = [s - h for s, h in zip(sums, high)]
    pad = jnp.zeros((LANES - 2 * experts, count), jnp.float32)
    table = jnp.concatenate(high + low + [pad], axis=0)
    table = jnp.concatenate([table, jnp.zeros((LANES, LANES - count), jnp.float32)], axis=1)
    w_ref[...] = table.T[:count]
    for place in range(2):
        weights = w_ref[pl.ds(starts[place], half), :].astype(jnp.bfloat16)
        all_ref[pl.ds(place * half, half), pl.ds(width, LANES)] = weights
        if place == 0:
            mine_ref[:, pl.ds(width, LANES)] = weights
    for copy in copies[3:]:
        copy.wait()


def prepare(tokens, gates, slots, plan, experts, attn_at, expert_at):
    count, width = tokens.shape
    top = slots.shape[1]
    given = [pltpu.with_memory_space_constraint(v, pltpu.HBM) for v in (plan, slots.T, gates.T, tokens)]
    return pl.pallas_call(
        functools.partial(prepare_kernel, experts),
        out_shape=(
            jax.ShapeDtypeStruct((count, width + LANES), jnp.bfloat16),
            jax.ShapeDtypeStruct((count // 2, width + LANES), jnp.bfloat16),
        ),
        in_specs=[SMEM] * 2 + [pl.BlockSpec(memory_space=pltpu.HBM)] * 4,
        out_specs=(VMEM, VMEM),
        scratch_shapes=[
            pltpu.SMEM((experts,), jnp.int32),
            pltpu.VMEM((top, count), jnp.int32),
            pltpu.VMEM((top, count), jnp.float32),
            pltpu.VMEM((count, LANES), jnp.float32),
            pltpu.SemaphoreType.DMA((6,)),
        ],
        compiler_params=pltpu.CompilerParams(vmem_limit_bytes=SMALL),
        name="prepare",
    )(attn_at.reshape(1), expert_at.reshape(1), *given)


def load_kernel(*refs):
    count = len(refs) // 2
    sources, targets, sems = refs[:count], refs[count : 2 * count], refs[-1]
    copies = [
        pltpu.make_async_copy(source, target, sems.at[i])
        for i, (source, target) in enumerate(zip(sources, targets))
    ]
    for copy in copies:
        copy.start()
    for copy in copies:
        copy.wait()


def load(*arrays):
    return pl.pallas_call(
        load_kernel,
        out_shape=tuple(jax.ShapeDtypeStruct(a.shape, a.dtype) for a in arrays),
        in_specs=[pl.BlockSpec(memory_space=pltpu.HBM)] * len(arrays),
        out_specs=(VMEM,) * len(arrays),
        scratch_shapes=[pltpu.SemaphoreType.DMA((len(arrays),))],
        compiler_params=pltpu.CompilerParams(vmem_limit_bytes=SMALL),
        cost_estimate=pl.CostEstimate(
            flops=0, transcendentals=0, bytes_accessed=sum(2 * a.size * a.dtype.itemsize for a in arrays)
        ),
        name="load",
    )(*[pltpu.with_memory_space_constraint(a, pltpu.HBM) for a in arrays])


def ffn_kernel(experts, blocks, at_ref, *refs):
    x_refs = refs[:blocks]
    gate_ref, up_ref, down_ref, keep_ref, send_ref, x_ref, h_ref, w_ref = refs[blocks:]
    width, units = gate_ref.shape
    row = 0
    for ref in x_refs:
        size = ref.shape[0]
        x_ref[pl.ds(row, size), :] = ref[:, pl.ds(0, width)]
        w_ref[pl.ds(row, size), :] = ref[:, pl.ds(width, LANES)].astype(jnp.float32)
        row += size
    lane = lax.broadcasted_iota(jnp.int32, (1, LANES), 1)
    own = (lane == at_ref[0]) | (lane == at_ref[0] + experts)
    weight = jnp.sum(jnp.where(own, w_ref[...], 0.0), axis=1, keepdims=True)
    w_ref[...] = jnp.broadcast_to(weight, w_ref.shape)
    tile = min(256, units)
    for n in range(0, units, tile):
        cols = pl.ds(n, tile)
        gate = jnp.dot(x_ref[...], gate_ref[:, cols], preferred_element_type=jnp.float32)
        up = jnp.dot(x_ref[...], up_ref[:, cols], preferred_element_type=jnp.float32)
        h_ref[:, cols] = (gate / (1.0 + jnp.exp(-gate)) * up).astype(jnp.bfloat16)
    half = row // 2
    wide = 512
    for start in range(0, width, wide):
        cols = pl.ds(start, min(wide, width - start))
        y = lax.dot_general(
            h_ref[...], down_ref[cols, :], (((1,), (1,)), ((), ())), preferred_element_type=jnp.float32
        )
        y = (y * w_ref[:, pl.ds(0, 1)]).astype(jnp.bfloat16)
        keep_ref[:, cols] = y[:half]
        send_ref[:, cols] = y[half:]


def ffn(x_blocks, w_gate, w_up, w_down, expert_at, experts):
    width, units = w_gate.shape
    rows = sum(b.shape[0] for b in x_blocks)
    out = jax.ShapeDtypeStruct((rows // 2, width), jnp.bfloat16)
    return pl.pallas_call(
        functools.partial(ffn_kernel, experts, len(x_blocks)),
        out_shape=(out, out),
        in_specs=[SMEM] + [VMEM] * (len(x_blocks) + 3),
        out_specs=(VMEM, VMEM),
        scratch_shapes=[
            pltpu.VMEM((rows, width), jnp.bfloat16),
            pltpu.VMEM((rows, units), jnp.bfloat16),
            pltpu.VMEM((rows, LANES), jnp.float32),
        ],
        cost_estimate=pl.CostEstimate(
            flops=6 * rows * width * units,
            bytes_accessed=6 * width * units + 8 * rows * width,
            transcendentals=rows * units,
        ),
        compiler_params=pltpu.CompilerParams(vmem_limit_bytes=2 * SMALL),
        name="ffn",
    )(expert_at.reshape(1), *x_blocks, w_gate, w_up, w_down)


def add(*terms):
    total = terms[0].astype(jnp.float32)
    for term in terms[1:]:
        total = total + term.astype(jnp.float32)
    return total.astype(jnp.bfloat16)


def body_line(tokens, gates, slots, plan, gate_proj, up_proj, down_proj):
    return line(tokens, gates, slots, plan, gate_proj, up_proj, down_proj)


def line(tokens, gates, slots, plan, gate_proj, up_proj, down_proj):
    experts = lax.axis_size("expert")
    expert_at = lax.axis_index("expert").astype(jnp.int32)
    attn_at = lax.axis_index("attn").astype(jnp.int32)
    count = tokens.shape[0]
    half = count // 2

    def swap(value, bit):
        return lax.ppermute(value, "expert", [(i, i ^ bit) for i in range(experts)])

    def core(value):
        return swap(value, 1)

    def pair(value):
        return lax.ppermute(value, "attn", [(0, 1), (1, 0)])

    def run(*blocks):
        return ffn(blocks, *weights, expert_at, experts)

    own, mine = prepare(tokens, gates, slots, plan, experts, attn_at, expert_at)
    far = swap(mine, 4)
    near = swap(own, 2)
    own_core = core(own)
    weights = load(gate_proj[0], up_proj[0], down_proj[0])
    near_core = core(near)
    keep, send = run(own, near, own_core, near_core)
    got = core(send)
    near_sum = swap(add(keep[count:], got[count:]), 2)
    both = add(keep[:count], got[:count], near_sum)

    far_pair = pair(far)
    blocks = (swap(far, 2), swap(far_pair, 2), far, far_pair)
    far_keep, far_send = run(*blocks, *[core(b) for b in blocks])
    far_got = core(far_send)
    total = [add(far_keep[i : i + half], far_got[i : i + half]) for i in range(0, 2 * count, half)]
    relay_other = pair(total[1])
    far_other = pair(total[3])
    near_other = pair(both[half:])
    relay_sum = swap(add(total[0], relay_other), 2)
    far_sum = swap(add(total[2], far_other, relay_sum), 4)
    final = add(both[:half], near_other, far_sum)
    other = pair(final)
    return jnp.where(
        attn_at == 0,
        jnp.concatenate([final, other], axis=0),
        jnp.concatenate([other, final], axis=0),
    )


def body_any(tokens, gates, slots, plan, gate_proj, up_proj, down_proj):
    experts = lax.axis_size("expert")
    expert_at = lax.axis_index("expert").astype(jnp.int32)
    owner = slots >> 1
    chosen = jnp.where((slots & 1) == 0, owner, plan[owner])
    hit = chosen[:, :, None] == jnp.arange(experts, dtype=jnp.int32)
    sums = jnp.sum(jnp.where(hit, gates[:, :, None], 0.0), axis=1)
    rows = lax.all_gather(tokens, "expert", axis=0, tiled=True)
    weight = lax.all_gather(sums, "expert", axis=0, tiled=True)
    weight = jnp.sum(
        jnp.where(jnp.arange(experts, dtype=jnp.int32) == expert_at, weight, 0.0), axis=1
    )
    gate = jnp.dot(rows, gate_proj[0], preferred_element_type=jnp.float32)
    up = jnp.dot(rows, up_proj[0], preferred_element_type=jnp.float32)
    hidden = (jax.nn.silu(gate) * up).astype(jnp.bfloat16)
    down = jnp.einsum("rf,df->rd", hidden, down_proj[0], preferred_element_type=jnp.float32)
    part = (down * weight[:, None]).astype(jnp.bfloat16)
    mine = lax.psum_scatter(part, "expert", scatter_dimension=0, tiled=True)
    return lax.psum(mine, "attn")


def solution(mesh):
    sizes = dict(mesh.shape)
    line_form = sizes["attn"] == 2 and sizes["expert"] == 8
    return jax.shard_map(
        body_line if line_form else body_any,
        mesh=mesh,
        in_specs=(
            P(("groups", "expert"), None),
            P(("groups", "expert"), None),
            P(("groups", "expert"), None),
            P("groups"),
            P("expert", None, "attn"),
            P("expert", None, "attn"),
            P("expert", None, "attn"),
        ),
        out_specs=P(("groups", "expert"), None),
        check_vma=False,
    )
```

```python
import functools

import jax
import jax.numpy as jnp
from jax import lax
from jax.experimental import pallas as pl
from jax.experimental.pallas import tpu as pltpu
from jax.sharding import PartitionSpec as P

LANES = 128
SMALL = 4 << 20
VMEM = pl.BlockSpec(memory_space=pltpu.VMEM)
SMEM = pl.BlockSpec(memory_space=pltpu.SMEM)


def expert_weights(slots, gates, plan_ref, experts):
    owner = slots >> 1
    copied = jnp.zeros_like(slots)
    for d in range(experts):
        copied = jnp.where(owner == d, plan_ref[d], copied)
    chosen = jnp.where((slots & 1) == 0, owner, copied)
    return [
        jnp.sum(jnp.where(chosen == e, gates, 0.0), axis=0, keepdims=True)
        for e in range(experts)
    ]


def prepare_kernel(
    experts, at_ref, expert_ref, plan_hbm, slots_hbm, gates_hbm, tok_hbm, all_ref, mine_ref,
    plan_ref, slots_ref, gates_ref, w_ref, sems
):
    count, width = tok_hbm.shape
    half = count // 2
    copies = [
        pltpu.make_async_copy(plan_hbm, plan_ref, sems.at[0]),
        pltpu.make_async_copy(slots_hbm, slots_ref, sems.at[1]),
        pltpu.make_async_copy(gates_hbm, gates_ref, sems.at[2]),
    ]
    starts = [pl.multiple_of((at_ref[0] ^ place) * half, half) for place in range(2)]
    targets = [
        (starts[0], mine_ref.at[:, pl.ds(0, width)]),
        (starts[0], all_ref.at[pl.ds(0, half), pl.ds(0, width)]),
        (starts[1], all_ref.at[pl.ds(half, half), pl.ds(0, width)]),
    ]
    for i, (start, target) in enumerate(targets):
        copies.append(pltpu.make_async_copy(tok_hbm.at[pl.ds(start, half), :], target, sems.at[3 + i]))
    for copy in copies:
        copy.start()
    for copy in copies[:3]:
        copy.wait()
    sums = expert_weights(slots_ref[...], gates_ref[...], plan_ref, experts)
    high = [s.astype(jnp.bfloat16).astype(jnp.float32) for s in sums]
    low = [s - h for s, h in zip(sums, high)]
    pad = jnp.zeros((LANES - 2 * experts, count), jnp.float32)
    table = jnp.concatenate(high + low + [pad], axis=0)
    table = jnp.concatenate([table, jnp.zeros((LANES, LANES - count), jnp.float32)], axis=1)
    w_ref[...] = table.T[:count]
    for place in range(2):
        weights = w_ref[pl.ds(starts[place], half), :].astype(jnp.bfloat16)
        all_ref[pl.ds(place * half, half), pl.ds(width, LANES)] = weights
        if place == 0:
            mine_ref[:, pl.ds(width, LANES)] = weights
    for copy in copies[3:]:
        copy.wait()


def prepare(tokens, gates, slots, plan, experts, attn_at, expert_at):
    count, width = tokens.shape
    top = slots.shape[1]
    given = [pltpu.with_memory_space_constraint(v, pltpu.HBM) for v in (plan, slots.T, gates.T, tokens)]
    return pl.pallas_call(
        functools.partial(prepare_kernel, experts),
        out_shape=(
            jax.ShapeDtypeStruct((count, width + LANES), jnp.bfloat16),
            jax.ShapeDtypeStruct((count // 2, width + LANES), jnp.bfloat16),
        ),
        in_specs=[SMEM] * 2 + [pl.BlockSpec(memory_space=pltpu.HBM)] * 4,
        out_specs=(VMEM, VMEM),
        scratch_shapes=[
            pltpu.SMEM((experts,), jnp.int32),
            pltpu.VMEM((top, count), jnp.int32),
            pltpu.VMEM((top, count), jnp.float32),
            pltpu.VMEM((count, LANES), jnp.float32),
            pltpu.SemaphoreType.DMA((6,)),
        ],
        compiler_params=pltpu.CompilerParams(vmem_limit_bytes=SMALL),
        name="prepare",
    )(attn_at.reshape(1), expert_at.reshape(1), *given)


def load_kernel(*refs):
    count = len(refs) // 2
    sources, targets, sems = refs[:count], refs[count : 2 * count], refs[-1]
    copies = [
        pltpu.make_async_copy(source, target, sems.at[i])
        for i, (source, target) in enumerate(zip(sources, targets))
    ]
    for copy in copies:
        copy.start()
    for copy in copies:
        copy.wait()


def load(*arrays):
    return pl.pallas_call(
        load_kernel,
        out_shape=tuple(jax.ShapeDtypeStruct(a.shape, a.dtype) for a in arrays),
        in_specs=[pl.BlockSpec(memory_space=pltpu.HBM)] * len(arrays),
        out_specs=(VMEM,) * len(arrays),
        scratch_shapes=[pltpu.SemaphoreType.DMA((len(arrays),))],
        compiler_params=pltpu.CompilerParams(vmem_limit_bytes=SMALL),
        cost_estimate=pl.CostEstimate(
            flops=0, transcendentals=0, bytes_accessed=sum(2 * a.size * a.dtype.itemsize for a in arrays)
        ),
        name="load",
    )(*[pltpu.with_memory_space_constraint(a, pltpu.HBM) for a in arrays])


def ffn_kernel(experts, blocks, at_ref, *refs):
    x_refs = refs[:blocks]
    gate_ref, up_ref, down_ref, keep_ref, send_ref, x_ref, h_ref, w_ref = refs[blocks:]
    width, units = gate_ref.shape
    row = 0
    for ref in x_refs:
        size = ref.shape[0]
        x_ref[pl.ds(row, size), :] = ref[:, pl.ds(0, width)]
        w_ref[pl.ds(row, size), :] = ref[:, pl.ds(width, LANES)].astype(jnp.float32)
        row += size
    lane = lax.broadcasted_iota(jnp.int32, (1, LANES), 1)
    own = (lane == at_ref[0]) | (lane == at_ref[0] + experts)
    weight = jnp.sum(jnp.where(own, w_ref[...], 0.0), axis=1, keepdims=True)
    w_ref[...] = jnp.broadcast_to(weight, w_ref.shape)
    tile = min(256, units)
    for n in range(0, units, tile):
        cols = pl.ds(n, tile)
        gate = jnp.dot(x_ref[...], gate_ref[:, cols], preferred_element_type=jnp.float32)
        up = jnp.dot(x_ref[...], up_ref[:, cols], preferred_element_type=jnp.float32)
        h_ref[:, cols] = (gate / (1.0 + jnp.exp(-gate)) * up).astype(jnp.bfloat16)
    half = row // 2
    wide = 512
    for start in range(0, width, wide):
        cols = pl.ds(start, min(wide, width - start))
        y = lax.dot_general(
            h_ref[...], down_ref[cols, :], (((1,), (1,)), ((), ())), preferred_element_type=jnp.float32
        )
        y = (y * w_ref[:, pl.ds(0, 1)]).astype(jnp.bfloat16)
        keep_ref[:, cols] = y[:half]
        send_ref[:, cols] = y[half:]


def ffn(x_blocks, w_gate, w_up, w_down, expert_at, experts):
    width, units = w_gate.shape
    rows = sum(b.shape[0] for b in x_blocks)
    out = jax.ShapeDtypeStruct((rows // 2, width), jnp.bfloat16)
    return pl.pallas_call(
        functools.partial(ffn_kernel, experts, len(x_blocks)),
        out_shape=(out, out),
        in_specs=[SMEM] + [VMEM] * (len(x_blocks) + 3),
        out_specs=(VMEM, VMEM),
        scratch_shapes=[
            pltpu.VMEM((rows, width), jnp.bfloat16),
            pltpu.VMEM((rows, units), jnp.bfloat16),
            pltpu.VMEM((rows, LANES), jnp.float32),
        ],
        cost_estimate=pl.CostEstimate(
            flops=6 * rows * width * units,
            bytes_accessed=6 * width * units + 8 * rows * width,
            transcendentals=rows * units,
        ),
        compiler_params=pltpu.CompilerParams(vmem_limit_bytes=2 * SMALL),
        name="ffn",
    )(expert_at.reshape(1), *x_blocks, w_gate, w_up, w_down)


def add(*terms):
    total = terms[0].astype(jnp.float32)
    for term in terms[1:]:
        total = total + term.astype(jnp.float32)
    return total.astype(jnp.bfloat16)


def body_line(tokens, gates, slots, plan, gate_proj, up_proj, down_proj):
    return line(tokens, gates, slots, plan, gate_proj, up_proj, down_proj)


def line(tokens, gates, slots, plan, gate_proj, up_proj, down_proj):
    experts = lax.axis_size("expert")
    expert_at = lax.axis_index("expert").astype(jnp.int32)
    attn_at = lax.axis_index("attn").astype(jnp.int32)
    count = tokens.shape[0]
    half = count // 2

    def swap(value, bit):
        return lax.ppermute(value, "expert", [(i, i ^ bit) for i in range(experts)])

    def core(value):
        return swap(value, 1)

    def pair(value):
        return lax.ppermute(value, "attn", [(0, 1), (1, 0)])

    def cross(value, bit):
        order = [(i, i ^ (2 * bit + 1)) for i in range(2 * experts)]
        return lax.ppermute(value, ("expert", "attn"), order)

    def run(*blocks):
        return ffn(blocks, *weights, expert_at, experts)

    own, mine = prepare(tokens, gates, slots, plan, experts, attn_at, expert_at)
    far = swap(mine, 4)
    near = swap(own, 2)
    own_core = core(own)
    weights = load(gate_proj[0], up_proj[0], down_proj[0])
    near_core = core(near)
    keep, send = run(own, near, own_core, near_core)
    got = core(send)
    near_sum = swap(add(keep[count:], got[count:]), 2)
    both = add(keep[:count], got[:count], near_sum)

    blocks = (far, pair(far), swap(far, 2), cross(far, 2))
    far_keep, far_send = run(*blocks, *[core(b) for b in blocks])
    far_got = core(far_send)
    parts = [add(far_keep[i : i + half], far_got[i : i + half]) for i in range(0, 2 * count, half)]
    cross_sum = cross(parts[3], 2)
    far_other = pair(parts[1])
    relay_sum = swap(parts[2], 2)
    far_sum = swap(add(parts[0], far_other, relay_sum, cross_sum), 4)
    near_other = pair(both[half:])
    final = add(both[:half], near_other, far_sum)
    other = pair(final)
    return jnp.where(
        attn_at == 0,
        jnp.concatenate([final, other], axis=0),
        jnp.concatenate([other, final], axis=0),
    )


def body_any(tokens, gates, slots, plan, gate_proj, up_proj, down_proj):
    experts = lax.axis_size("expert")
    expert_at = lax.axis_index("expert").astype(jnp.int32)
    owner = slots >> 1
    chosen = jnp.where((slots & 1) == 0, owner, plan[owner])
    hit = chosen[:, :, None] == jnp.arange(experts, dtype=jnp.int32)
    sums = jnp.sum(jnp.where(hit, gates[:, :, None], 0.0), axis=1)
    rows = lax.all_gather(tokens, "expert", axis=0, tiled=True)
    weight = lax.all_gather(sums, "expert", axis=0, tiled=True)
    weight = jnp.sum(
        jnp.where(jnp.arange(experts, dtype=jnp.int32) == expert_at, weight, 0.0), axis=1
    )
    gate = jnp.dot(rows, gate_proj[0], preferred_element_type=jnp.float32)
    up = jnp.dot(rows, up_proj[0], preferred_element_type=jnp.float32)
    hidden = (jax.nn.silu(gate) * up).astype(jnp.bfloat16)
    down = jnp.einsum("rf,df->rd", hidden, down_proj[0], preferred_element_type=jnp.float32)
    part = (down * weight[:, None]).astype(jnp.bfloat16)
    mine = lax.psum_scatter(part, "expert", scatter_dimension=0, tiled=True)
    return lax.psum(mine, "attn")


def solution(mesh):
    sizes = dict(mesh.shape)
    line_form = sizes["attn"] == 2 and sizes["expert"] == 8
    return jax.shard_map(
        body_line if line_form else body_any,
        mesh=mesh,
        in_specs=(
            P(("groups", "expert"), None),
            P(("groups", "expert"), None),
            P(("groups", "expert"), None),
            P("groups"),
            P("expert", None, "attn"),
            P("expert", None, "attn"),
            P("expert", None, "attn"),
        ),
        out_specs=P(("groups", "expert"), None),
        check_vma=False,
    )
```

```python
import functools

import jax
import jax.numpy as jnp
from jax import lax
from jax.experimental import pallas as pl
from jax.experimental.pallas import tpu as pltpu
from jax.sharding import PartitionSpec as P

LANES = 128
SMALL = 4 << 20
VMEM = pl.BlockSpec(memory_space=pltpu.VMEM)
SMEM = pl.BlockSpec(memory_space=pltpu.SMEM)


def expert_weights(slots, gates, plan_ref, experts):
    owner = slots >> 1
    copied = jnp.zeros_like(slots)
    for d in range(experts):
        copied = jnp.where(owner == d, plan_ref[d], copied)
    chosen = jnp.where((slots & 1) == 0, owner, copied)
    return [
        jnp.sum(jnp.where(chosen == e, gates, 0.0), axis=0, keepdims=True)
        for e in range(experts)
    ]


def prepare_kernel(
    experts, at_ref, expert_ref, plan_hbm, slots_hbm, gates_hbm, tok_hbm, all_ref, mine_ref,
    plan_ref, slots_ref, gates_ref, w_ref, sems
):
    count, width = tok_hbm.shape
    half = count // 2
    copies = [
        pltpu.make_async_copy(plan_hbm, plan_ref, sems.at[0]),
        pltpu.make_async_copy(slots_hbm, slots_ref, sems.at[1]),
        pltpu.make_async_copy(gates_hbm, gates_ref, sems.at[2]),
    ]
    starts = [pl.multiple_of((at_ref[0] ^ place) * half, half) for place in range(2)]
    targets = [
        (starts[0], mine_ref.at[:, pl.ds(0, width)]),
        (starts[0], all_ref.at[pl.ds(0, half), pl.ds(0, width)]),
        (starts[1], all_ref.at[pl.ds(half, half), pl.ds(0, width)]),
    ]
    for i, (start, target) in enumerate(targets):
        copies.append(pltpu.make_async_copy(tok_hbm.at[pl.ds(start, half), :], target, sems.at[3 + i]))
    for copy in copies:
        copy.start()
    for copy in copies[:3]:
        copy.wait()
    sums = expert_weights(slots_ref[...], gates_ref[...], plan_ref, experts)
    high = [s.astype(jnp.bfloat16).astype(jnp.float32) for s in sums]
    low = [s - h for s, h in zip(sums, high)]
    pad = jnp.zeros((LANES - 2 * experts, count), jnp.float32)
    table = jnp.concatenate(high + low + [pad], axis=0)
    table = jnp.concatenate([table, jnp.zeros((LANES, LANES - count), jnp.float32)], axis=1)
    w_ref[...] = table.T[:count]
    for place in range(2):
        weights = w_ref[pl.ds(starts[place], half), :].astype(jnp.bfloat16)
        all_ref[pl.ds(place * half, half), pl.ds(width, LANES)] = weights
        if place == 0:
            mine_ref[:, pl.ds(width, LANES)] = weights
    for copy in copies[3:]:
        copy.wait()


def prepare(tokens, gates, slots, plan, experts, attn_at, expert_at):
    count, width = tokens.shape
    top = slots.shape[1]
    given = [pltpu.with_memory_space_constraint(v, pltpu.HBM) for v in (plan, slots.T, gates.T, tokens)]
    return pl.pallas_call(
        functools.partial(prepare_kernel, experts),
        out_shape=(
            jax.ShapeDtypeStruct((count, width + LANES), jnp.bfloat16),
            jax.ShapeDtypeStruct((count // 2, width + LANES), jnp.bfloat16),
        ),
        in_specs=[SMEM] * 2 + [pl.BlockSpec(memory_space=pltpu.HBM)] * 4,
        out_specs=(VMEM, VMEM),
        scratch_shapes=[
            pltpu.SMEM((experts,), jnp.int32),
            pltpu.VMEM((top, count), jnp.int32),
            pltpu.VMEM((top, count), jnp.float32),
            pltpu.VMEM((count, LANES), jnp.float32),
            pltpu.SemaphoreType.DMA((6,)),
        ],
        compiler_params=pltpu.CompilerParams(vmem_limit_bytes=SMALL),
        name="prepare",
    )(attn_at.reshape(1), expert_at.reshape(1), *given)


def load_kernel(gate_hbm, up_hbm, down_hbm, gate_ref, up_ref, down_ref, rows_ref, sems):
    width = down_hbm.shape[0]
    part = width // 2 if width % (2 * LANES) == 0 else width
    parts = range(0, width, part)
    copies = [
        pltpu.make_async_copy(
            down_hbm.at[pl.ds(at, part), :], rows_ref.at[pl.ds(at, part), :], sems.at[2 + i]
        )
        for i, at in enumerate(parts)
    ]
    others = [
        pltpu.make_async_copy(gate_hbm, gate_ref, sems.at[0]),
        pltpu.make_async_copy(up_hbm, up_ref, sems.at[1]),
    ]
    for copy in copies + others:
        copy.start()
    for copy, at in zip(copies, parts):
        copy.wait()
        tile = 256 if part % 256 == 0 else LANES
        for row in range(at, at + part, tile):
            down_ref[:, pl.ds(row, tile)] = rows_ref[pl.ds(row, tile), :].T
    for copy in others:
        copy.wait()


def load(gate, up, down):
    given = (gate, up, down)
    return pl.pallas_call(
        load_kernel,
        out_shape=(
            jax.ShapeDtypeStruct(gate.shape, gate.dtype),
            jax.ShapeDtypeStruct(up.shape, up.dtype),
            jax.ShapeDtypeStruct(down.shape[::-1], down.dtype),
        ),
        in_specs=[pl.BlockSpec(memory_space=pltpu.HBM)] * 3,
        out_specs=(VMEM,) * 3,
        scratch_shapes=[pltpu.VMEM(down.shape, down.dtype), pltpu.SemaphoreType.DMA((4,))],
        compiler_params=pltpu.CompilerParams(vmem_limit_bytes=2 * SMALL),
        cost_estimate=pl.CostEstimate(
            flops=0, transcendentals=0, bytes_accessed=sum(2 * a.size * a.dtype.itemsize for a in given)
        ),
        name="load",
    )(*[pltpu.with_memory_space_constraint(a, pltpu.HBM) for a in given])


def ffn_kernel(experts, blocks, at_ref, *refs):
    x_refs = refs[:blocks]
    gate_ref, up_ref, down_ref, keep_ref, send_ref, x_ref, h_ref, w_ref = refs[blocks:]
    width, units = gate_ref.shape
    row = 0
    for ref in x_refs:
        size = ref.shape[0]
        x_ref[pl.ds(row, size), :] = ref[:, pl.ds(0, width)]
        w_ref[pl.ds(row, size), :] = ref[:, pl.ds(width, LANES)].astype(jnp.float32)
        row += size
    lane = lax.broadcasted_iota(jnp.int32, (1, LANES), 1)
    own = (lane == at_ref[0]) | (lane == at_ref[0] + experts)
    weight = jnp.sum(jnp.where(own, w_ref[...], 0.0), axis=1, keepdims=True)
    w_ref[...] = jnp.broadcast_to(weight, w_ref.shape)
    tile = min(256, units)
    for n in range(0, units, tile):
        cols = pl.ds(n, tile)
        gate = jnp.dot(x_ref[...], gate_ref[:, cols], preferred_element_type=jnp.float32)
        up = jnp.dot(x_ref[...], up_ref[:, cols], preferred_element_type=jnp.float32)
        h_ref[:, cols] = (gate / (1.0 + jnp.exp(-gate)) * up).astype(jnp.bfloat16)
    half = row // 2
    wide = 512
    for start in range(0, width, wide):
        cols = pl.ds(start, min(wide, width - start))
        y = jnp.dot(h_ref[...], down_ref[:, cols], preferred_element_type=jnp.float32)
        y = (y * w_ref[:, pl.ds(0, 1)]).astype(jnp.bfloat16)
        keep_ref[:, cols] = y[:half]
        send_ref[:, cols] = y[half:]


def ffn(x_blocks, w_gate, w_up, w_down, expert_at, experts):
    width, units = w_gate.shape
    rows = sum(b.shape[0] for b in x_blocks)
    out = jax.ShapeDtypeStruct((rows // 2, width), jnp.bfloat16)
    return pl.pallas_call(
        functools.partial(ffn_kernel, experts, len(x_blocks)),
        out_shape=(out, out),
        in_specs=[SMEM] + [VMEM] * (len(x_blocks) + 3),
        out_specs=(VMEM, VMEM),
        scratch_shapes=[
            pltpu.VMEM((rows, width), jnp.bfloat16),
            pltpu.VMEM((rows, units), jnp.bfloat16),
            pltpu.VMEM((rows, LANES), jnp.float32),
        ],
        cost_estimate=pl.CostEstimate(
            flops=6 * rows * width * units,
            bytes_accessed=6 * width * units + 8 * rows * width,
            transcendentals=rows * units,
        ),
        compiler_params=pltpu.CompilerParams(vmem_limit_bytes=2 * SMALL),
        name="ffn",
    )(expert_at.reshape(1), *x_blocks, w_gate, w_up, w_down)


def add(*terms):
    total = terms[0].astype(jnp.float32)
    for term in terms[1:]:
        total = total + term.astype(jnp.float32)
    return total.astype(jnp.bfloat16)


def body_line(tokens, gates, slots, plan, gate_proj, up_proj, down_proj):
    return line(tokens, gates, slots, plan, gate_proj, up_proj, down_proj)


def line(tokens, gates, slots, plan, gate_proj, up_proj, down_proj):
    experts = lax.axis_size("expert")
    expert_at = lax.axis_index("expert").astype(jnp.int32)
    attn_at = lax.axis_index("attn").astype(jnp.int32)
    count = tokens.shape[0]
    half = count // 2

    def swap(value, bit):
        return lax.ppermute(value, "expert", [(i, i ^ bit) for i in range(experts)])

    def core(value):
        return swap(value, 1)

    def pair(value):
        return lax.ppermute(value, "attn", [(0, 1), (1, 0)])

    def cross(value, bit):
        order = [(i, i ^ (2 * bit + 1)) for i in range(2 * experts)]
        return lax.ppermute(value, ("expert", "attn"), order)

    def run(*blocks):
        return ffn(blocks, *weights, expert_at, experts)

    own, mine = prepare(tokens, gates, slots, plan, experts, attn_at, expert_at)
    far = swap(mine, 4)
    near = swap(own, 2)
    own_core = core(own)
    weights = load(gate_proj[0], up_proj[0], down_proj[0])
    near_core = core(near)
    keep, send = run(own, near, own_core, near_core)
    got = core(send)
    near_sum = swap(add(keep[count:], got[count:]), 2)
    both = add(keep[:count], got[:count], near_sum)

    blocks = (far, pair(far), swap(far, 2), cross(far, 2))
    far_keep, far_send = run(*blocks, *[core(b) for b in blocks])
    far_got = core(far_send)
    parts = [add(far_keep[i : i + half], far_got[i : i + half]) for i in range(0, 2 * count, half)]
    cross_sum = cross(parts[3], 2)
    far_other = pair(parts[1])
    relay_sum = swap(parts[2], 2)
    far_sum = swap(add(parts[0], far_other, relay_sum, cross_sum), 4)
    near_other = pair(both[half:])
    final = add(both[:half], near_other, far_sum)
    other = pair(final)
    return jnp.where(
        attn_at == 0,
        jnp.concatenate([final, other], axis=0),
        jnp.concatenate([other, final], axis=0),
    )


def body_any(tokens, gates, slots, plan, gate_proj, up_proj, down_proj):
    experts = lax.axis_size("expert")
    expert_at = lax.axis_index("expert").astype(jnp.int32)
    owner = slots >> 1
    chosen = jnp.where((slots & 1) == 0, owner, plan[owner])
    hit = chosen[:, :, None] == jnp.arange(experts, dtype=jnp.int32)
    sums = jnp.sum(jnp.where(hit, gates[:, :, None], 0.0), axis=1)
    rows = lax.all_gather(tokens, "expert", axis=0, tiled=True)
    weight = lax.all_gather(sums, "expert", axis=0, tiled=True)
    weight = jnp.sum(
        jnp.where(jnp.arange(experts, dtype=jnp.int32) == expert_at, weight, 0.0), axis=1
    )
    gate = jnp.dot(rows, gate_proj[0], preferred_element_type=jnp.float32)
    up = jnp.dot(rows, up_proj[0], preferred_element_type=jnp.float32)
    hidden = (jax.nn.silu(gate) * up).astype(jnp.bfloat16)
    down = jnp.einsum("rf,df->rd", hidden, down_proj[0], preferred_element_type=jnp.float32)
    part = (down * weight[:, None]).astype(jnp.bfloat16)
    mine = lax.psum_scatter(part, "expert", scatter_dimension=0, tiled=True)
    return lax.psum(mine, "attn")


def solution(mesh):
    sizes = dict(mesh.shape)
    line_form = sizes["attn"] == 2 and sizes["expert"] == 8
    return jax.shard_map(
        body_line if line_form else body_any,
        mesh=mesh,
        in_specs=(
            P(("groups", "expert"), None),
            P(("groups", "expert"), None),
            P(("groups", "expert"), None),
            P("groups"),
            P("expert", None, "attn"),
            P("expert", None, "attn"),
            P("expert", None, "attn"),
        ),
        out_specs=P(("groups", "expert"), None),
        check_vma=False,
    )
```

```python
import functools

import jax
import jax.numpy as jnp
from jax import lax
from jax.experimental import pallas as pl
from jax.experimental.pallas import tpu as pltpu
from jax.sharding import PartitionSpec as P

LANES = 128
SMALL = 4 << 20
VMEM = pl.BlockSpec(memory_space=pltpu.VMEM)
SMEM = pl.BlockSpec(memory_space=pltpu.SMEM)


def expert_weights(slots, gates, plan_ref, experts):
    owner = slots >> 1
    copied = jnp.zeros_like(slots)
    for d in range(experts):
        copied = jnp.where(owner == d, plan_ref[d], copied)
    chosen = jnp.where((slots & 1) == 0, owner, copied)
    return [
        jnp.sum(jnp.where(chosen == e, gates, 0.0), axis=0, keepdims=True)
        for e in range(experts)
    ]


def prepare_kernel(
    experts, at_ref, expert_ref, plan_hbm, slots_hbm, gates_hbm, tok_hbm, all_ref, mine_ref,
    plan_ref, slots_ref, gates_ref, w_ref, sems
):
    count, width = tok_hbm.shape
    half = count // 2
    copies = [
        pltpu.make_async_copy(plan_hbm, plan_ref, sems.at[0]),
        pltpu.make_async_copy(slots_hbm, slots_ref, sems.at[1]),
        pltpu.make_async_copy(gates_hbm, gates_ref, sems.at[2]),
    ]
    starts = [pl.multiple_of((at_ref[0] ^ place) * half, half) for place in range(2)]
    targets = [
        (starts[0], mine_ref.at[:, pl.ds(0, width)]),
        (starts[0], all_ref.at[pl.ds(0, half), pl.ds(0, width)]),
        (starts[1], all_ref.at[pl.ds(half, half), pl.ds(0, width)]),
    ]
    for i, (start, target) in enumerate(targets):
        copies.append(pltpu.make_async_copy(tok_hbm.at[pl.ds(start, half), :], target, sems.at[3 + i]))
    for copy in copies:
        copy.start()
    for copy in copies[:3]:
        copy.wait()
    sums = expert_weights(slots_ref[...], gates_ref[...], plan_ref, experts)
    high = [s.astype(jnp.bfloat16).astype(jnp.float32) for s in sums]
    low = [s - h for s, h in zip(sums, high)]
    pad = jnp.zeros((LANES - 2 * experts, count), jnp.float32)
    table = jnp.concatenate(high + low + [pad], axis=0)
    table = jnp.concatenate([table, jnp.zeros((LANES, LANES - count), jnp.float32)], axis=1)
    w_ref[...] = table.T[:count]
    for place in range(2):
        weights = w_ref[pl.ds(starts[place], half), :].astype(jnp.bfloat16)
        all_ref[pl.ds(place * half, half), pl.ds(width, LANES)] = weights
        if place == 0:
            mine_ref[:, pl.ds(width, LANES)] = weights
    for copy in copies[3:]:
        copy.wait()


def prepare(tokens, gates, slots, plan, experts, attn_at, expert_at):
    count, width = tokens.shape
    top = slots.shape[1]
    given = [pltpu.with_memory_space_constraint(v, pltpu.HBM) for v in (plan, slots.T, gates.T, tokens)]
    return pl.pallas_call(
        functools.partial(prepare_kernel, experts),
        out_shape=(
            jax.ShapeDtypeStruct((count, width + LANES), jnp.bfloat16),
            jax.ShapeDtypeStruct((count // 2, width + LANES), jnp.bfloat16),
        ),
        in_specs=[SMEM] * 2 + [pl.BlockSpec(memory_space=pltpu.HBM)] * 4,
        out_specs=(VMEM, VMEM),
        scratch_shapes=[
            pltpu.SMEM((experts,), jnp.int32),
            pltpu.VMEM((top, count), jnp.int32),
            pltpu.VMEM((top, count), jnp.float32),
            pltpu.VMEM((count, LANES), jnp.float32),
            pltpu.SemaphoreType.DMA((6,)),
        ],
        compiler_params=pltpu.CompilerParams(vmem_limit_bytes=SMALL),
        name="prepare",
    )(attn_at.reshape(1), expert_at.reshape(1), *given)


def load_kernel(gate_hbm, up_hbm, down_hbm, gate_ref, up_ref, down_ref, rows_ref, sems):
    width = down_hbm.shape[0]
    part = width // 2 if width % (2 * LANES) == 0 else width
    parts = range(0, width, part)
    copies = [
        pltpu.make_async_copy(
            down_hbm.at[pl.ds(at, part), :], rows_ref.at[pl.ds(at, part), :], sems.at[2 + i]
        )
        for i, at in enumerate(parts)
    ]
    others = [
        pltpu.make_async_copy(gate_hbm, gate_ref, sems.at[0]),
        pltpu.make_async_copy(up_hbm, up_ref, sems.at[1]),
    ]
    for copy in copies + others:
        copy.start()
    for copy, at in zip(copies, parts):
        copy.wait()
        tile = 256 if part % 256 == 0 else LANES
        for row in range(at, at + part, tile):
            down_ref[:, pl.ds(row, tile)] = rows_ref[pl.ds(row, tile), :].T
    for copy in others:
        copy.wait()


def load(gate, up, down):
    given = (gate, up, down)
    return pl.pallas_call(
        load_kernel,
        out_shape=(
            jax.ShapeDtypeStruct(gate.shape, gate.dtype),
            jax.ShapeDtypeStruct(up.shape, up.dtype),
            jax.ShapeDtypeStruct(down.shape[::-1], down.dtype),
        ),
        in_specs=[pl.BlockSpec(memory_space=pltpu.HBM)] * 3,
        out_specs=(VMEM,) * 3,
        scratch_shapes=[pltpu.VMEM(down.shape, down.dtype), pltpu.SemaphoreType.DMA((4,))],
        compiler_params=pltpu.CompilerParams(vmem_limit_bytes=2 * SMALL),
        cost_estimate=pl.CostEstimate(
            flops=0, transcendentals=0, bytes_accessed=sum(2 * a.size * a.dtype.itemsize for a in given)
        ),
        name="load",
    )(*[pltpu.with_memory_space_constraint(a, pltpu.HBM) for a in given])


def ffn_kernel(experts, blocks, at_ref, *refs):
    x_refs = refs[:blocks]
    gate_ref, up_ref, down_ref, keep_ref, send_ref, x_ref, h_ref, w_ref = refs[blocks:]
    width, units = gate_ref.shape
    row = 0
    for ref in x_refs:
        size = ref.shape[0]
        x_ref[pl.ds(row, size), :] = ref[:, pl.ds(0, width)]
        w_ref[pl.ds(row, size), :] = ref[:, pl.ds(width, LANES)].astype(jnp.float32)
        row += size
    lane = lax.broadcasted_iota(jnp.int32, (1, LANES), 1)
    own = (lane == at_ref[0]) | (lane == at_ref[0] + experts)
    weight = jnp.sum(jnp.where(own, w_ref[...], 0.0), axis=1, keepdims=True)
    w_ref[...] = jnp.broadcast_to(weight, w_ref.shape)
    tile = min(256, units)
    for n in range(0, units, tile):
        cols = pl.ds(n, tile)
        gate = jnp.dot(x_ref[...], gate_ref[:, cols], preferred_element_type=jnp.float32)
        up = jnp.dot(x_ref[...], up_ref[:, cols], preferred_element_type=jnp.float32)
        h_ref[:, cols] = (gate / (1.0 + jnp.exp(-gate)) * up).astype(jnp.bfloat16)
    half = row // 2
    wide = 512
    for start in range(0, width, wide):
        cols = pl.ds(start, min(wide, width - start))
        y = jnp.dot(h_ref[...], down_ref[:, cols], preferred_element_type=jnp.float32)
        y = (y * w_ref[:, pl.ds(0, 1)]).astype(jnp.bfloat16)
        keep_ref[:, cols] = y[:half]
        send_ref[:, cols] = y[half:]


def ffn(x_blocks, w_gate, w_up, w_down, expert_at, experts):
    width, units = w_gate.shape
    rows = sum(b.shape[0] for b in x_blocks)
    out = jax.ShapeDtypeStruct((rows // 2, width), jnp.bfloat16)
    return pl.pallas_call(
        functools.partial(ffn_kernel, experts, len(x_blocks)),
        out_shape=(out, out),
        in_specs=[SMEM] + [VMEM] * (len(x_blocks) + 3),
        out_specs=(VMEM, VMEM),
        scratch_shapes=[
            pltpu.VMEM((rows, width), jnp.bfloat16),
            pltpu.VMEM((rows, units), jnp.bfloat16),
            pltpu.VMEM((rows, LANES), jnp.float32),
        ],
        cost_estimate=pl.CostEstimate(
            flops=6 * rows * width * units,
            bytes_accessed=6 * width * units + 8 * rows * width,
            transcendentals=rows * units,
        ),
        compiler_params=pltpu.CompilerParams(vmem_limit_bytes=2 * SMALL),
        name="ffn",
    )(expert_at.reshape(1), *x_blocks, w_gate, w_up, w_down)


def add(*terms):
    total = terms[0].astype(jnp.float32)
    for term in terms[1:]:
        total = total + term.astype(jnp.float32)
    return total.astype(jnp.bfloat16)


def body_line(tokens, gates, slots, plan, gate_proj, up_proj, down_proj):
    return line(tokens, gates, slots, plan, gate_proj, up_proj, down_proj)


def line(tokens, gates, slots, plan, gate_proj, up_proj, down_proj):
    experts = lax.axis_size("expert")
    expert_at = lax.axis_index("expert").astype(jnp.int32)
    attn_at = lax.axis_index("attn").astype(jnp.int32)
    count = tokens.shape[0]
    half = count // 2

    def swap(value, bit):
        return lax.ppermute(value, "expert", [(i, i ^ bit) for i in range(experts)])

    def core(value):
        return swap(value, 1)

    def pair(value):
        return lax.ppermute(value, "attn", [(0, 1), (1, 0)])

    def cross(value, bit):
        order = [(i, i ^ (2 * bit + 1)) for i in range(2 * experts)]
        return lax.ppermute(value, ("expert", "attn"), order)

    def run(*blocks):
        return ffn(blocks, *weights, expert_at, experts)

    own, mine = prepare(tokens, gates, slots, plan, experts, attn_at, expert_at)
    far = swap(mine, 4)
    near = swap(own, 2)
    own_core = core(own)
    weights = load(gate_proj[0], up_proj[0], down_proj[0])
    near_core = core(near)
    far_core = core(far)
    keep, send = run(own, near, far, own_core, near_core, far_core)
    got = core(send)
    near_sum = swap(add(keep[count:], got[count:]), 2)
    both = add(keep[:count], got[:count], near_sum[:count])

    blocks = (pair(far), swap(far, 2), cross(far, 2))
    far_keep, far_send = run(*blocks, *[core(b) for b in blocks])
    far_got = core(far_send)
    parts = [add(far_keep[i : i + half], far_got[i : i + half]) for i in range(0, 3 * half, half)]
    far_other = pair(parts[2])
    cross_sum = cross(parts[0], 2)
    far_sum = swap(add(parts[1], far_other, near_sum[count:], cross_sum), 6)
    near_other = pair(both[half:])
    final = add(both[:half], near_other, far_sum)
    other = pair(final)
    result = jnp.zeros((count, final.shape[1]), final.dtype)
    result = lax.dynamic_update_slice(result, final, (attn_at * half, 0))
    return lax.dynamic_update_slice(result, other, ((1 - attn_at) * half, 0))


def body_any(tokens, gates, slots, plan, gate_proj, up_proj, down_proj):
    experts = lax.axis_size("expert")
    expert_at = lax.axis_index("expert").astype(jnp.int32)
    owner = slots >> 1
    chosen = jnp.where((slots & 1) == 0, owner, plan[owner])
    hit = chosen[:, :, None] == jnp.arange(experts, dtype=jnp.int32)
    sums = jnp.sum(jnp.where(hit, gates[:, :, None], 0.0), axis=1)
    rows = lax.all_gather(tokens, "expert", axis=0, tiled=True)
    weight = lax.all_gather(sums, "expert", axis=0, tiled=True)
    weight = jnp.sum(
        jnp.where(jnp.arange(experts, dtype=jnp.int32) == expert_at, weight, 0.0), axis=1
    )
    gate = jnp.dot(rows, gate_proj[0], preferred_element_type=jnp.float32)
    up = jnp.dot(rows, up_proj[0], preferred_element_type=jnp.float32)
    hidden = (jax.nn.silu(gate) * up).astype(jnp.bfloat16)
    down = jnp.einsum("rf,df->rd", hidden, down_proj[0], preferred_element_type=jnp.float32)
    part = (down * weight[:, None]).astype(jnp.bfloat16)
    mine = lax.psum_scatter(part, "expert", scatter_dimension=0, tiled=True)
    return lax.psum(mine, "attn")


def solution(mesh):
    sizes = dict(mesh.shape)
    line_form = sizes["attn"] == 2 and sizes["expert"] == 8
    return jax.shard_map(
        body_line if line_form else body_any,
        mesh=mesh,
        in_specs=(
            P(("groups", "expert"), None),
            P(("groups", "expert"), None),
            P(("groups", "expert"), None),
            P("groups"),
            P("expert", None, "attn"),
            P("expert", None, "attn"),
            P("expert", None, "attn"),
        ),
        out_specs=P(("groups", "expert"), None),
        check_vma=False,
    )
```

```python
import functools

import jax
import jax.numpy as jnp
from jax import lax
from jax.experimental import pallas as pl
from jax.experimental.pallas import tpu as pltpu
from jax.sharding import PartitionSpec as P

LANES = 128
SMALL = 4 << 20
VMEM = pl.BlockSpec(memory_space=pltpu.VMEM)
SMEM = pl.BlockSpec(memory_space=pltpu.SMEM)


def expert_weights(slots, gates, plan_ref, experts):
    owner = slots >> 1
    copied = jnp.zeros_like(slots)
    for d in range(experts):
        copied = jnp.where(owner == d, plan_ref[d], copied)
    chosen = jnp.where((slots & 1) == 0, owner, copied)
    return [
        jnp.sum(jnp.where(chosen == e, gates, 0.0), axis=0, keepdims=True)
        for e in range(experts)
    ]


def prepare_kernel(
    experts, at_ref, expert_ref, plan_hbm, slots_hbm, gates_hbm, tok_hbm, all_ref, mine_ref,
    plan_ref, slots_ref, gates_ref, w_ref, sems
):
    count, width = tok_hbm.shape
    half = count // 2
    copies = [
        pltpu.make_async_copy(plan_hbm, plan_ref, sems.at[0]),
        pltpu.make_async_copy(slots_hbm, slots_ref, sems.at[1]),
        pltpu.make_async_copy(gates_hbm, gates_ref, sems.at[2]),
    ]
    starts = [pl.multiple_of((at_ref[0] ^ place) * half, half) for place in range(2)]
    targets = [
        (starts[0], mine_ref.at[:, pl.ds(0, width)]),
        (starts[0], all_ref.at[pl.ds(0, half), pl.ds(0, width)]),
        (starts[1], all_ref.at[pl.ds(half, half), pl.ds(0, width)]),
    ]
    for i, (start, target) in enumerate(targets):
        copies.append(pltpu.make_async_copy(tok_hbm.at[pl.ds(start, half), :], target, sems.at[3 + i]))
    for copy in copies:
        copy.start()
    for copy in copies[:3]:
        copy.wait()
    sums = expert_weights(slots_ref[...], gates_ref[...], plan_ref, experts)
    high = [s.astype(jnp.bfloat16).astype(jnp.float32) for s in sums]
    low = [s - h for s, h in zip(sums, high)]
    pad = jnp.zeros((LANES - 2 * experts, count), jnp.float32)
    table = jnp.concatenate(high + low + [pad], axis=0)
    table = jnp.concatenate([table, jnp.zeros((LANES, LANES - count), jnp.float32)], axis=1)
    w_ref[...] = table.T[:count]
    for place in range(2):
        weights = w_ref[pl.ds(starts[place], half), :].astype(jnp.bfloat16)
        all_ref[pl.ds(place * half, half), pl.ds(width, LANES)] = weights
        if place == 0:
            mine_ref[:, pl.ds(width, LANES)] = weights
    for copy in copies[3:]:
        copy.wait()


def prepare(tokens, gates, slots, plan, experts, attn_at, expert_at):
    count, width = tokens.shape
    top = slots.shape[1]
    given = [pltpu.with_memory_space_constraint(v, pltpu.HBM) for v in (plan, slots.T, gates.T, tokens)]
    return pl.pallas_call(
        functools.partial(prepare_kernel, experts),
        out_shape=(
            jax.ShapeDtypeStruct((count, width + LANES), jnp.bfloat16),
            jax.ShapeDtypeStruct((count // 2, width + LANES), jnp.bfloat16),
        ),
        in_specs=[SMEM] * 2 + [pl.BlockSpec(memory_space=pltpu.HBM)] * 4,
        out_specs=(VMEM, VMEM),
        scratch_shapes=[
            pltpu.SMEM((experts,), jnp.int32),
            pltpu.VMEM((top, count), jnp.int32),
            pltpu.VMEM((top, count), jnp.float32),
            pltpu.VMEM((count, LANES), jnp.float32),
            pltpu.SemaphoreType.DMA((6,)),
        ],
        compiler_params=pltpu.CompilerParams(vmem_limit_bytes=SMALL),
        name="prepare",
    )(attn_at.reshape(1), expert_at.reshape(1), *given)


def load_kernel(gate_hbm, up_hbm, down_hbm, gate_ref, up_ref, down_ref, rows_ref, sems):
    width = down_hbm.shape[0]
    part = width // 2 if width % (2 * LANES) == 0 else width
    parts = range(0, width, part)
    copies = [
        pltpu.make_async_copy(
            down_hbm.at[pl.ds(at, part), :], rows_ref.at[pl.ds(at, part), :], sems.at[2 + i]
        )
        for i, at in enumerate(parts)
    ]
    others = [
        pltpu.make_async_copy(gate_hbm, gate_ref, sems.at[0]),
        pltpu.make_async_copy(up_hbm, up_ref, sems.at[1]),
    ]
    for copy in copies + others:
        copy.start()
    for copy, at in zip(copies, parts):
        copy.wait()
        tile = 256 if part % 256 == 0 else LANES
        for row in range(at, at + part, tile):
            down_ref[:, pl.ds(row, tile)] = rows_ref[pl.ds(row, tile), :].T
    for copy in others:
        copy.wait()


def load(gate, up, down):
    given = (gate, up, down)
    return pl.pallas_call(
        load_kernel,
        out_shape=(
            jax.ShapeDtypeStruct(gate.shape, gate.dtype),
            jax.ShapeDtypeStruct(up.shape, up.dtype),
            jax.ShapeDtypeStruct(down.shape[::-1], down.dtype),
        ),
        in_specs=[pl.BlockSpec(memory_space=pltpu.HBM)] * 3,
        out_specs=(VMEM,) * 3,
        scratch_shapes=[pltpu.VMEM(down.shape, down.dtype), pltpu.SemaphoreType.DMA((4,))],
        compiler_params=pltpu.CompilerParams(vmem_limit_bytes=2 * SMALL),
        cost_estimate=pl.CostEstimate(
            flops=0, transcendentals=0, bytes_accessed=sum(2 * a.size * a.dtype.itemsize for a in given)
        ),
        name="load",
    )(*[pltpu.with_memory_space_constraint(a, pltpu.HBM) for a in given])


def ffn_kernel(experts, blocks, at_ref, *refs):
    x_refs = refs[:blocks]
    gate_ref, up_ref, down_ref, keep_ref, send_ref, x_ref, h_ref, w_ref = refs[blocks:]
    width, units = gate_ref.shape
    row = 0
    for ref in x_refs:
        size = ref.shape[0]
        x_ref[pl.ds(row, size), :] = ref[:, pl.ds(0, width)]
        w_ref[pl.ds(row, size), :] = ref[:, pl.ds(width, LANES)].astype(jnp.float32)
        row += size
    spare = x_ref.shape[0] - row
    if spare:
        x_ref[pl.ds(row, spare), :] = jnp.zeros((spare, width), x_ref.dtype)
        w_ref[pl.ds(row, spare), :] = jnp.zeros((spare, LANES), w_ref.dtype)
    lane = lax.broadcasted_iota(jnp.int32, (1, LANES), 1)
    own = (lane == at_ref[0]) | (lane == at_ref[0] + experts)
    weight = jnp.sum(jnp.where(own, w_ref[...], 0.0), axis=1, keepdims=True)
    w_ref[...] = jnp.broadcast_to(weight, w_ref.shape)
    tile = min(256, units)
    for n in range(0, units, tile):
        cols = pl.ds(n, tile)
        gate = jnp.dot(x_ref[...], gate_ref[:, cols], preferred_element_type=jnp.float32)
        up = jnp.dot(x_ref[...], up_ref[:, cols], preferred_element_type=jnp.float32)
        h_ref[:, cols] = (gate / (1.0 + jnp.exp(-gate)) * up).astype(jnp.bfloat16)
    half = row // 2
    wide = 512
    for start in range(0, width, wide):
        cols = pl.ds(start, min(wide, width - start))
        y = jnp.dot(h_ref[...], down_ref[:, cols], preferred_element_type=jnp.float32)
        y = (y * w_ref[:, pl.ds(0, 1)]).astype(jnp.bfloat16)
        keep_ref[:, cols] = y[:half]
        send_ref[:, cols] = y[half:row]


def ffn(x_blocks, w_gate, w_up, w_down, expert_at, experts):
    width, units = w_gate.shape
    rows = sum(b.shape[0] for b in x_blocks)
    out = jax.ShapeDtypeStruct((rows // 2, width), jnp.bfloat16)
    return pl.pallas_call(
        functools.partial(ffn_kernel, experts, len(x_blocks)),
        out_shape=(out, out),
        in_specs=[SMEM] + [VMEM] * (len(x_blocks) + 3),
        out_specs=(VMEM, VMEM),
        scratch_shapes=[
            pltpu.VMEM((max(rows, LANES), width), jnp.bfloat16),
            pltpu.VMEM((max(rows, LANES), units), jnp.bfloat16),
            pltpu.VMEM((max(rows, LANES), LANES), jnp.float32),
        ],
        cost_estimate=pl.CostEstimate(
            flops=6 * rows * width * units,
            bytes_accessed=6 * width * units + 8 * rows * width,
            transcendentals=rows * units,
        ),
        compiler_params=pltpu.CompilerParams(vmem_limit_bytes=2 * SMALL),
        name="ffn",
    )(expert_at.reshape(1), *x_blocks, w_gate, w_up, w_down)


def add(*terms):
    total = terms[0].astype(jnp.float32)
    for term in terms[1:]:
        total = total + term.astype(jnp.float32)
    return total.astype(jnp.bfloat16)


def body_line(tokens, gates, slots, plan, gate_proj, up_proj, down_proj):
    return line(tokens, gates, slots, plan, gate_proj, up_proj, down_proj)


def line(tokens, gates, slots, plan, gate_proj, up_proj, down_proj):
    experts = lax.axis_size("expert")
    expert_at = lax.axis_index("expert").astype(jnp.int32)
    attn_at = lax.axis_index("attn").astype(jnp.int32)
    count = tokens.shape[0]
    half = count // 2

    def swap(value, bit):
        return lax.ppermute(value, "expert", [(i, i ^ bit) for i in range(experts)])

    def core(value):
        return swap(value, 1)

    def pair(value):
        return lax.ppermute(value, "attn", [(0, 1), (1, 0)])

    def cross(value, bit):
        order = [(i, i ^ (2 * bit + 1)) for i in range(2 * experts)]
        return lax.ppermute(value, ("expert", "attn"), order)

    def run(*blocks):
        return ffn(blocks, *weights, expert_at, experts)

    own, mine = prepare(tokens, gates, slots, plan, experts, attn_at, expert_at)
    far = swap(mine, 4)
    near = swap(own, 2)
    own_core = core(own)
    weights = load(gate_proj[0], up_proj[0], down_proj[0])
    near_core = core(near)
    far_core = core(far)
    keep, send = run(own, near, far, own_core, near_core, far_core)
    got = core(send)
    near_sum = swap(add(keep[count:], got[count:]), 2)
    both = add(keep[:count], got[:count], near_sum[:count])

    blocks = (pair(far), swap(far, 2), cross(far, 2))
    far_keep, far_send = run(*blocks, *[core(b) for b in blocks])
    far_got = core(far_send)
    parts = [add(far_keep[i : i + half], far_got[i : i + half]) for i in range(0, 3 * half, half)]
    far_other = pair(parts[2])
    cross_sum = cross(parts[0], 2)
    far_sum = swap(add(parts[1], far_other, near_sum[count:], cross_sum), 6)
    near_other = pair(both[half:])
    final = add(both[:half], near_other, far_sum)
    other = pair(final)
    result = jnp.zeros((count, final.shape[1]), final.dtype)
    result = lax.dynamic_update_slice(result, final, (attn_at * half, 0))
    return lax.dynamic_update_slice(result, other, ((1 - attn_at) * half, 0))


def body_any(tokens, gates, slots, plan, gate_proj, up_proj, down_proj):
    experts = lax.axis_size("expert")
    expert_at = lax.axis_index("expert").astype(jnp.int32)
    owner = slots >> 1
    chosen = jnp.where((slots & 1) == 0, owner, plan[owner])
    hit = chosen[:, :, None] == jnp.arange(experts, dtype=jnp.int32)
    sums = jnp.sum(jnp.where(hit, gates[:, :, None], 0.0), axis=1)
    rows = lax.all_gather(tokens, "expert", axis=0, tiled=True)
    weight = lax.all_gather(sums, "expert", axis=0, tiled=True)
    weight = jnp.sum(
        jnp.where(jnp.arange(experts, dtype=jnp.int32) == expert_at, weight, 0.0), axis=1
    )
    gate = jnp.dot(rows, gate_proj[0], preferred_element_type=jnp.float32)
    up = jnp.dot(rows, up_proj[0], preferred_element_type=jnp.float32)
    hidden = (jax.nn.silu(gate) * up).astype(jnp.bfloat16)
    down = jnp.einsum("rf,df->rd", hidden, down_proj[0], preferred_element_type=jnp.float32)
    part = (down * weight[:, None]).astype(jnp.bfloat16)
    mine = lax.psum_scatter(part, "expert", scatter_dimension=0, tiled=True)
    return lax.psum(mine, "attn")


def solution(mesh):
    sizes = dict(mesh.shape)
    line_form = sizes["attn"] == 2 and sizes["expert"] == 8
    return jax.shard_map(
        body_line if line_form else body_any,
        mesh=mesh,
        in_specs=(
            P(("groups", "expert"), None),
            P(("groups", "expert"), None),
            P(("groups", "expert"), None),
            P("groups"),
            P("expert", None, "attn"),
            P("expert", None, "attn"),
            P("expert", None, "attn"),
        ),
        out_specs=P(("groups", "expert"), None),
        check_vma=False,
    )
```
